32 devices in a mesh: fsdp: 8 (over y, x, core), cp: 4 (over z).
Axes of the slice: x: 2, y: 2, z: 4, core: 2. Of those that a mesh axis runs over, the one named last changes fastest.
Arguments:
- hidden: float32 [8, 512, 1536], P('fsdp', 'cp'), may hold values from -6 to 6
- d_out: float32 [8, 512, 1536], P('fsdp', 'cp'), may hold values from -6 to 6
- seg_ids: int32 [8, 512], P('fsdp', 'cp'), may hold values from 0 to 3, never falling along the last dimension, each value on 1 to 256 neighbouring positions
- w_in: bfloat16 [2, 1536, 6448], P(None, 'fsdp', 'cp'), may hold values from -0.15625 to 0.15625
- w_out: bfloat16 [2, 3072, 1536], P(None, 'fsdp', 'cp'), may hold values from -0.109375 to 0.109375
- norm_in: float32 [2, 1536], replicated, may hold values from 0.5 to 1.5
- norm_gate: float32 [2, 3072], replicated, may hold values from 0.5 to 1.5
- conv_w: float32 [2, 4, 3328], replicated, may hold values from -3 to 3
- conv_b: float32 [2, 3328], replicated, may hold values from -2 to 2
- dt_bias: float32 [2, 48], replicated, may hold values from -2 to 0
- a_log: float32 [2, 48], replicated, may hold values from -5.8 to -1.9
- d_skip: float32 [2, 48], replicated, may hold values from 0.5 to 1.5
Outputs:
- activations: float32 [8, 512, 1536], P('fsdp', 'cp')
- d_hidden: float32 [8, 512, 1536], P('fsdp', 'cp')
- grad_w_in: float32 [2, 1536, 6448], P(None, 'fsdp', 'cp')
- grad_w_out: float32 [2, 3072, 1536], P(None, 'fsdp', 'cp')
- grad_norm_in: float32 [2, 1536], replicated
- grad_norm_gate: float32 [2, 3072], replicated
- grad_conv_w: float32 [2, 4, 3328], replicated
- grad_conv_b: float32 [2, 3328], replicated
- grad_dt_bias: float32 [2, 48], replicated
- grad_a_log: float32 [2, 48], replicated
- grad_d_skip: float32 [2, 48], replicated
The draws below stay inside these ranges and needn't reach their ends.
Inputs may be any that keep to these rules, and one draw needn't show every extreme that they name: `seg_ids`: within each sequence the ids never fall; each id marks one document of at most half of 512 tokens, and every id appears.
All inputs are finite; a program needn't handle non-finite values.
Results may differ from the reference program's by a relative error of at most 0.0093.
Values may be sent and summed in bfloat16 or wider, within the bound.
No kernel may reach another device: no remote copies, remote signals or barrier semaphores. Data moves between devices by JAX's collectives and lax.ppermute only.
A program may use at most 320 MiB of HBM per device.

```python
import math
import jax
import jax.numpy as jnp
import numpy as np
from jax import lax

D = 1536
HEADS = 48
HEADDIM = 64
STATE = 128
CONV = 4
LAYERS = 2
INNER = 3072
CHANNELS = 3328
PROJ = 6448
GROUP = 128
SEQLEN = 512
BATCH = 8


def shard_levels(stream_key, dims, shards, smallest, top_value):
    loudness = 1.0
    for dim, parts in shards:
        heights = jax.random.uniform(jax.random.fold_in(jax.random.fold_in(stream_key, 6), dim), (parts,), jnp.float32, smallest / len(shards), top_value / len(shards))
        loudness = loudness * jnp.repeat(jnp.exp(heights), dims[dim] // parts).reshape((-1,) + (1,) * (len(dims) - 1 - dim))
    return loudness


def length_profile(count, total, bound, slope):
    loads = [(1 << 20) // math.isqrt(rank ** slope) + 1 for rank in range(2, count + 1)]
    rest, counts = total - bound - (count - 1), [1] * (count - 1)
    while rest > 0:
        candidates = [i for i in range(count - 1) if counts[i] < bound]
        whole, left = sum([loads[i] for i in candidates]), rest
        for i in candidates:
            addition = min(bound - counts[i], max(1, left * loads[i] // whole), rest)
            counts[i] = counts[i] + addition
            rest = rest - addition
    return np.array([bound] + counts)


def ragged_sizes(rng, number_of, total, most, slope):
    if number_of == 2:
        one = jax.random.randint(rng, (), max(1, total - most), min(most, total - 1) + 1)
        return jnp.stack([one, total - one])
    sizes = jnp.asarray(length_profile(number_of, total, most, slope), jnp.int32)
    pairs = (number_of - 1) // 2
    giver, taker = sizes[1:1 + 2 * pairs:2], sizes[2:2 + 2 * pairs:2]
    margin = jnp.minimum(giver - 1, most - taker)
    shifted = jax.random.randint(jax.random.fold_in(rng, 1), (pairs,), 0, 1 << 20) % (margin + 1)
    sizes = sizes.at[1:1 + 2 * pairs:2].set(giver - shifted).at[2:2 + 2 * pairs:2].set(taker + shifted)
    return sizes[jax.random.permutation(jax.random.fold_in(rng, 2), number_of)]


def gaussian(stream_key, dims, scale, reach, pieces=(), dtype=jnp.bfloat16):
    loudness = shard_levels(stream_key, dims, pieces, -0.22, 0.18) if pieces else 1.0
    drawn = jax.random.normal(stream_key, dims, jnp.float32) * scale * loudness
    return jnp.minimum(jnp.maximum(drawn, -reach), reach).astype(dtype)


def setup_inputs(seed: int = 0) -> dict:
    arg_keys = jax.random.split(jax.random.key(seed), 13)
    hidden = gaussian(arg_keys[0], (BATCH, SEQLEN, D), 1.0, 6.0, ((0, 8), (1, 4)), jnp.float32)
    d_out = gaussian(arg_keys[1], (BATCH, SEQLEN, D), 1.0, 6.0, ((0, 8), (1, 4)), jnp.float32)
    seg_ids = jax.vmap(lambda own: jnp.searchsorted(jnp.cumsum(ragged_sizes(own, 4, SEQLEN, SEQLEN // 2, 0)), jnp.arange(SEQLEN), side="right"))(jax.random.split(arg_keys[2], BATCH)).reshape((BATCH, SEQLEN)).astype(jnp.int32)
    w_in = gaussian(arg_keys[3], (LAYERS, D, PROJ), D ** -0.5, 0.15625, ((1, 8), (2, 4)))
    w_out = gaussian(arg_keys[4], (LAYERS, INNER, D), INNER ** -0.5, 0.109375, ((1, 8), (2, 4)))
    norm_in = jnp.clip(1.0 + 0.1 * jax.random.normal(arg_keys[5], (LAYERS, D), jnp.float32), 0.5, 1.5)
    norm_gate = jnp.clip(1.0 + 0.1 * jax.random.normal(arg_keys[6], (LAYERS, INNER), jnp.float32), 0.5, 1.5)
    conv_w = gaussian(arg_keys[7], (LAYERS, CONV, CHANNELS), CONV ** -0.5, 3.0, (), jnp.float32)
    conv_b = gaussian(arg_keys[8], (LAYERS, CHANNELS), 0.3, 2.0, (), jnp.float32)
    dt_bias = jnp.clip(jax.random.uniform(arg_keys[9], (LAYERS, HEADS), jnp.float32, -2.0, 0.0), -2.0, 0.0)
    a_log = jnp.clip(jax.random.uniform(arg_keys[10], (LAYERS, HEADS), jnp.float32, -5.8, -1.9), -5.8, -1.9)
    d_skip = jnp.clip(jax.random.uniform(arg_keys[11], (LAYERS, HEADS), jnp.float32, 0.5, 1.5), 0.5, 1.5)
    return dict(hidden=hidden, d_out=d_out, seg_ids=seg_ids, w_in=w_in, w_out=w_out, norm_in=norm_in, norm_gate=norm_gate, conv_w=conv_w, conv_b=conv_b, dt_bias=dt_bias, a_log=a_log, d_skip=d_skip)


EPSILON = 1e-05
FULL = lax.Precision.HIGHEST

@jax.custom_vjp
def low(v):
    return lax.optimization_barrier(v.astype(jnp.bfloat16)).astype(jnp.float32)

@jax.custom_vjp
def low_back(v):
    return v

def low_keep(v):
    return (low(v), None)

def low_pass(kept, grad):
    return (grad,)

def back_keep(v):
    return (v, None)

def back_low(kept, grad):
    return (low(grad),)
low.defvjp(low_keep, low_pass)
low_back.defvjp(back_keep, back_low)

def rms_norm(values, gain_vec):
    return values * lax.rsqrt(lax.optimization_barrier(jnp.mean(values * values, axis=-1, keepdims=True)) + EPSILON) * gain_vec

def conv_mix(padded, seg_pad, weight_taps, bias_vec):
    count_rows = padded.shape[-2] - CONV + 1
    target = seg_pad[..., CONV - 1:]
    summed = bias_vec
    for offset in range(CONV):
        window = padded[..., offset:offset + count_rows, :]
        match_mask = (seg_pad[..., offset:offset + count_rows] == target).astype(jnp.float32)
        summed = summed + weight_taps[offset] * window * match_mask[..., None]
    return jax.nn.silu(summed)

def group_step(decay_rate, carried, block_in):
    state_now, prev_seg = carried
    inputs, step_size, b_rows, c_rows, seg_now = block_in
    length_now = seg_now.shape[0]
    cumul = jnp.cumsum(step_size * decay_rate, axis=0)
    positions = jnp.arange(length_now)
    same_seg = jnp.logical_and(seg_now[:, None] == seg_now[None, :], positions[:, None] >= positions[None, :]).astype(jnp.float32)[:, :, None]
    spread = cumul[:, None, :] - cumul[None, :, :]
    lower_mask = jnp.exp(jnp.where(same_seg > 0, spread, 0.0)) * same_seg
    scores = jnp.dot(c_rows, b_rows.T, precision=FULL)
    mixing = scores[:, :, None] * lower_mask * step_size[None, :, :]
    within = jnp.einsum('tsh,shp->thp', mixing, inputs, precision=FULL)
    keep_mask = (seg_now == prev_seg).astype(jnp.float32)
    into_scale = jnp.exp(cumul) * keep_mask[:, None]
    carried_out = jnp.einsum('tn,hpn->thp', c_rows, state_now, precision=FULL) * into_scale[:, :, None]
    tail_mask = (seg_now == seg_now[-1]).astype(jnp.float32)
    weight_s = jnp.exp(cumul[-1][None, :] - cumul) * tail_mask[:, None] * step_size
    fresh = jnp.einsum('shp,sn->hpn', inputs * weight_s[:, :, None], b_rows, precision=FULL)
    new_state = state_now * (jnp.exp(cumul[-1]) * keep_mask[-1])[:, None, None] + fresh
    return ((new_state, seg_now[-1]), within + carried_out)

def ssd_scan(inputs, step_size, decay_rate, b_rows, c_rows, seg_now, prev_seg):
    total_len = seg_now.shape[0]
    blocks = total_len // GROUP

    def advance(carried, block_in):
        return jax.checkpoint(group_step)(decay_rate, carried, block_in)
    shaped = (inputs.reshape(blocks, GROUP, HEADS, HEADDIM), step_size.reshape(blocks, GROUP, HEADS), b_rows.reshape(blocks, GROUP, STATE), c_rows.reshape(blocks, GROUP, STATE), seg_now.reshape(blocks, GROUP))
    zero_state = jnp.zeros((HEADS, HEADDIM, STATE), jnp.float32)
    final_carry, outputs = lax.scan(advance, (zero_state, prev_seg), shaped)
    return (outputs.reshape(total_len, HEADS, HEADDIM), final_carry[0])

def gate_norm(ssd_out, gate_z, norm_gate):
    flat_out = ssd_out.reshape(gate_z.shape) * jax.nn.silu(gate_z)
    return rms_norm(flat_out, norm_gate)

def layer_forward(hidden_seq, seg_seq, params):
    w_in, w_out, norm_in, norm_gate, conv_w, conv_b, dt_bias, a_log, d_skip = params
    normed = low(rms_norm(hidden_seq, norm_in))
    project = low_back(jnp.dot(normed, w_in, precision=FULL))
    gate_z = project[:, :INNER]
    xbc_raw = project[:, INNER:INNER + CHANNELS]
    dt_raw = project[:, INNER + CHANNELS:]
    padded = jnp.concatenate([jnp.zeros((CONV - 1, CHANNELS), jnp.float32), xbc_raw], axis=0)
    seg_pad = jnp.concatenate([jnp.full((CONV - 1,), -1.0, jnp.float32), seg_seq])
    mixed = conv_mix(padded, seg_pad, conv_w, conv_b)
    inputs = mixed[:, :INNER].reshape(-1, HEADS, HEADDIM)
    b_rows = mixed[:, INNER:INNER + STATE]
    c_rows = mixed[:, INNER + STATE:]
    step_size = jax.nn.softplus(dt_raw + dt_bias)
    decay_rate = -jnp.exp(a_log)
    ssd_out, final_state = ssd_scan(inputs, step_size, decay_rate, b_rows, c_rows, seg_seq, seg_seq[0])
    ssd_out = ssd_out + d_skip[:, None] * inputs
    gated = low(gate_norm(ssd_out, gate_z, norm_gate))
    branch = low_back(jnp.dot(gated, w_out, precision=FULL))
    return hidden_seq + branch

def forward(hidden, params, seg_f):

    def one_sequence(pair_in):
        hidden_seq, seg_seq = pair_in
        for layer_index in range(LAYERS):
            hidden_seq = layer_forward(hidden_seq, seg_seq, tuple((param[layer_index] for param in params)))
        return hidden_seq
    return lax.map(jax.checkpoint(one_sequence), (hidden, seg_f))

def reference(hidden, d_out, seg_ids, w_in, w_out, norm_in, norm_gate, conv_w, conv_b, dt_bias, a_log, d_skip):
    seg_f = seg_ids.astype(jnp.float32)
    params = (w_in.astype(jnp.float32), w_out.astype(jnp.float32), norm_in, norm_gate, conv_w, conv_b, dt_bias, a_log, d_skip)

    def run_layers(hidden_in, params_in):
        return forward(hidden_in, params_in, seg_f)
    outputs, pullback = jax.vjp(run_layers, hidden, params)
    grad_hidden, grad_params = pullback(d_out)
    return (outputs, grad_hidden, grad_params[0], grad_params[1], grad_params[2], grad_params[3], grad_params[4], grad_params[5], grad_params[6], grad_params[7], grad_params[8])
```

```python
import functools

import jax
import jax.numpy as jnp
from jax import lax
from jax.experimental import pallas as pl
from jax.experimental.pallas import tpu as pltpu
from jax.sharding import PartitionSpec as P


HEADS = 48
HEADDIM = 64
STATE = 128
LAYERS = 2
INNER = 3072
CHANNELS = 3328
PROJ = 6448
GROUP = 128
EPSILON = 1e-05
LANES = 128
ROWS = 32

F32 = jnp.float32
BF16 = jnp.bfloat16


def mm(a, b, ca, cb, precision=None):
    return lax.dot_general(
        a, b, (((ca,), (cb,)), ((), ())), precision=precision, preferred_element_type=F32
    )


def parts_of(v):
    high = v.astype(BF16)
    return high, (v - high.astype(F32)).astype(BF16)


def fine(a, b, ca, cb):
    return mm(a[0], b[0], ca, cb) + (mm(a[0], b[1], ca, cb) + mm(a[1], b[0], ca, cb))


def by_mask(v, ex, cb):
    high, low = parts_of(v)
    return mm(high, ex, 1, cb) + mm(low, ex, 1, cb)


def summed_rows(tri, v, ca):
    high = v.astype(BF16)
    rest = v - high.astype(F32)
    middle = rest.astype(BF16)
    low = (rest - middle.astype(F32)).astype(BF16)
    return mm(tri, high, ca, 0) + (mm(tri, middle, ca, 0) + mm(tri, low, ca, 0))


def sigmoid(v):
    return 1.0 / (1.0 + jnp.exp(-v))


def conv_parts(p_ref, prev_ref, ext, meta, cw_ref, hp):
    wide = hp + 2 * STATE
    raw = p_ref[:, hp : hp + wide]
    ext[0:8, :] = prev_ref[:, hp : hp + wide]
    ext[8 : 8 + GROUP, :] = raw
    pre = cw_ref[4:5, :] + cw_ref[3:4, :] * raw
    taps = [raw]
    for back in (1, 2, 3):
        shifted = ext[8 - back : 8 - back + GROUP, :]
        taps.append(shifted)
        pre = pre + cw_ref[3 - back : 4 - back, :] * shifted * meta[:, back - 1 : back]
    return pre, taps


def decay_parts(p_ref, meta, dtp_ref, hp):
    u = p_ref[:, 2 * hp + 2 * STATE :] + dtp_ref[0:1, :]
    dt = jnp.maximum(u, 0.0) + jnp.log1p(jnp.exp(-jnp.abs(u)))
    rows = lax.broadcasted_iota(jnp.int32, (GROUP, GROUP), 0)
    cols = lax.broadcasted_iota(jnp.int32, (GROUP, GROUP), 1)
    lower = rows >= cols
    tri = lower.astype(F32).astype(BF16)
    cum = summed_rows(tri, dt * dtp_ref[1:2, :], 1)
    last = cum[GROUP - 1 : GROUP, :]
    into = jnp.exp(cum) * meta[:, 3:4]
    tail = jnp.exp(last - cum) * meta[:, 4:5]
    through = jnp.exp(last) * meta[0:1, 6:7]
    return u, dt, cum, into, tail, through, lower, tri, rows


def fwd_kernel(
    base_ref, p_ref, prev_ref, meta_ref, seg_ref, cw_ref, dtp_ref, chp_ref, ex_ref,
    rg_ref, y_ref, st_ref, state, ext, *, hp, nh, cps,
):
    j = pl.program_id(0)

    @pl.when(lax.rem(j, cps) == 0)
    def _():
        state[...] = jnp.zeros_like(state)

    meta = meta_ref[...]
    pre, _ = conv_parts(p_ref, prev_ref, ext, meta, cw_ref, hp)
    mixed = pre * sigmoid(pre)
    x = mixed[:, :hp]
    b_rows = parts_of(mixed[:, hp : hp + STATE])
    c_rows = parts_of(mixed[:, hp + STATE :])
    _, dt, cum, into, tail, through, lower, _, _ = decay_parts(p_ref, meta, dtp_ref, hp)
    cum_t = cum.T
    dt_t = dt.T
    scores = fine(c_rows, b_rows, 1, 1)
    same = jnp.logical_and(lower, meta[:, 5:6] == seg_ref[0:1, :])
    ex = ex_ref[...]
    into_x = by_mask(into, ex, 0)
    weight_x = by_mask(tail * dt, ex, 0)
    through_x = by_mask(jnp.broadcast_to(through, (8, LANES)), ex, 0)[0:1, :]
    old = state[...]
    st_ref[0] = old
    carried = fine(c_rows, parts_of(old), 1, 0) * into_x
    state[...] = old * through_x + fine(b_rows, parts_of(x * weight_x), 0, 0)
    low_half = lax.broadcasted_iota(jnp.int32, (GROUP, LANES), 1) < HEADDIM
    total = jnp.zeros((GROUP, LANES), F32)
    for pair in range(nh // 2):
        at = slice(pair * LANES, (pair + 1) * LANES)
        xp = x[:, at]
        xb = parts_of(xp)
        halves = []
        for h in (2 * pair, 2 * pair + 1):
            spread = cum[:, h : h + 1] - cum_t[h : h + 1, :]
            mixing = scores * jnp.exp(jnp.where(same, spread, -1e30)) * dt_t[h : h + 1, :]
            halves.append(fine(parts_of(mixing), xb, 1, 0))
        y = jnp.where(low_half, halves[0], halves[1]) + carried[:, at] + chp_ref[0:1, at] * xp
        y_ref[:, at] = y
        z = p_ref[:, at]
        r = y * (z * sigmoid(z))
        rg_ref[:, at] = (r * chp_ref[1:2, at]).astype(BF16)
        total = total + r * r
    rg_ref[:, hp:] = total.astype(BF16)


def bwd_kernel(
    base_ref, p_ref, prev_ref, meta_ref, seg_ref, cw_ref, dtp_ref, chp_ref, ex_ref,
    y_ref, st_ref, gx_ref,
    gp_ref, gated_ref, gcw_ref, gch_ref, gdt_ref,
    dstate, ext, edge, row_sums, *, hp, nh, cps,
):
    step = pl.program_id(0)
    j = pl.num_programs(0) - 1 - step

    @pl.when(step == 0)
    def _():
        gcw_ref[...] = jnp.zeros_like(gcw_ref)
        gch_ref[...] = jnp.zeros_like(gch_ref)
        gdt_ref[...] = jnp.zeros_like(gdt_ref)
        row_sums[...] = jnp.zeros_like(row_sums)

    @pl.when(lax.rem(j, cps) == cps - 1)
    def _():
        dstate[...] = jnp.zeros_like(dstate)
        edge[...] = jnp.zeros_like(edge)

    meta = meta_ref[...]
    pre, taps = conv_parts(p_ref, prev_ref, ext, meta, cw_ref, hp)
    sig = sigmoid(pre)
    mixed = pre * sig
    x = mixed[:, :hp]
    b_rows = parts_of(mixed[:, hp : hp + STATE])
    c_rows = parts_of(mixed[:, hp + STATE :])
    u, dt, cum, into, tail, through, lower, tri, rows = decay_parts(p_ref, meta, dtp_ref, hp)
    cum_t = cum.T
    dt_t = dt.T
    scores = fine(c_rows, b_rows, 1, 1)
    same = jnp.logical_and(lower, meta[:, 5:6] == seg_ref[0:1, :])
    ex = ex_ref[...]
    weight = tail * dt
    into_x = by_mask(into, ex, 0)
    weight_x = by_mask(weight, ex, 0)
    through_x = by_mask(jnp.broadcast_to(through, (8, LANES)), ex, 0)[0:1, :]

    scal = gx_ref[:, hp:]
    inv = scal[:, 0:1] + scal[:, 1:2]
    pull = (scal[:, 2:3] + scal[:, 3:4]) * inv * inv * (1.0 / INNER)
    low_half = lax.broadcasted_iota(jnp.int32, (GROUP, LANES), 1) < HEADDIM
    lane = lax.broadcasted_iota(jnp.int32, (GROUP, LANES), 1)
    dys = []
    for pair in range(nh // 2):
        at = slice(pair * LANES, (pair + 1) * LANES)
        z, y, g = p_ref[:, at], y_ref[:, at], gx_ref[:, at]
        gain = chp_ref[1:2, at]
        sz = sigmoid(z)
        silu = z * sz
        r = y * silu
        scaled = r * inv
        gated_ref[:, at] = (scaled * gain).astype(BF16)
        gch_ref[1:2, at] += jnp.sum(g * scaled, axis=0, keepdims=True)
        dr = inv * (g * gain) - r * pull
        dys.append(dr * silu)
        gp_ref[:, at] = (dr * y * (sz * (1.0 + z * (1.0 - sz)))).astype(BF16)
    dy = jnp.concatenate(dys, axis=1)

    old = st_ref[0]
    after = dstate[...]
    old_b, after_b = parts_of(old), parts_of(after)
    dxw = fine(b_rows, after_b, 1, 0)
    dx_wide = dxw * weight_x + chp_ref[0:1, :] * dy
    db = fine(parts_of(x * weight_x), after_b, 1, 1)
    dye = parts_of(dy * into_x)
    dc = fine(dye, old_b, 1, 1)
    dweight = by_mask(dxw * x, ex, 1)
    dinto = by_mask(dy * fine(c_rows, old_b, 1, 0), ex, 1)
    dthrough = by_mask(
        jnp.broadcast_to(jnp.sum(old * after, axis=0, keepdims=True), (8, hp)), ex, 1
    )[0:1, :]
    dstate[...] = after * through_x + fine(c_rows, dye, 0, 0)
    gch_ref[0:1, :] += jnp.sum(dy * x, axis=0, keepdims=True)

    dscores = jnp.zeros((GROUP, GROUP), F32)
    row_part = jnp.zeros((GROUP, LANES), F32)
    dx_parts = []
    for pair in range(nh // 2):
        at = slice(pair * LANES, (pair + 1) * LANES)
        xb = parts_of(x[:, at])
        dyb = parts_of(dy[:, at])
        halves = []
        for side in (0, 1):
            h = 2 * pair + side
            mine = low_half if side == 0 else jnp.logical_not(low_half)
            spread = cum[:, h : h + 1] - cum_t[h : h + 1, :]
            decay = jnp.exp(jnp.where(same, spread, -1e30))
            dtr = dt_t[h : h + 1, :]
            decayed = scores * decay
            mixing = parts_of(decayed * dtr)
            dmix = fine([jnp.where(mine, v, jnp.zeros_like(v)) for v in dyb], xb, 1, 1)
            dscores = dscores + dmix * decay * dtr
            flow = dmix * decayed
            row_sums[h : h + 1, :] = jnp.sum(flow, axis=0, keepdims=True)
            across = jnp.sum(flow * dtr, axis=1, keepdims=True)
            row_part = jnp.where(lane == h, across, row_part)
            halves.append(fine(mixing, dyb, 0, 0))
        dx_parts.append(jnp.where(low_half, halves[0], halves[1]))
    dx_wide = dx_wide + jnp.concatenate(dx_parts, axis=1)
    dsb = parts_of(dscores)
    db = db + fine(dsb, c_rows, 0, 0)
    dc = dc + fine(dsb, b_rows, 1, 0)

    col_part = row_sums[...].T
    used = dweight * weight
    at_last = jnp.sum(used, axis=0, keepdims=True) + dthrough * through
    dcum = row_part + dinto * into - dt * col_part - used
    dcum = dcum + jnp.where(rows == GROUP - 1, at_last, 0.0)
    dstep = summed_rows(tri, dcum, 0)
    ddt = col_part + dweight * tail + dstep * dtp_ref[1:2, :]
    du = ddt * sigmoid(u)
    gdt_ref[0:1, :] += jnp.sum(du, axis=0, keepdims=True)
    gdt_ref[1:2, :] += jnp.sum(dstep * dt, axis=0, keepdims=True)
    gp_ref[:, 2 * hp + 2 * STATE :] = du.astype(BF16)

    dmixed = jnp.concatenate([dx_wide, db, dc], axis=1)
    dpre = dmixed * (sig * (1.0 + pre * (1.0 - sig)))
    gcw_ref[4:5, :] += jnp.sum(dpre, axis=0, keepdims=True)
    gcw_ref[3:4, :] += jnp.sum(dpre * taps[0], axis=0, keepdims=True)
    draw = cw_ref[3:4, :] * dpre
    masked_all = []
    for back in (1, 2, 3):
        masked = dpre * meta[:, back - 1 : back]
        gcw_ref[3 - back : 4 - back, :] += jnp.sum(masked * taps[back], axis=0, keepdims=True)
        masked_all.append(masked)
    for back in (1, 2, 3):
        masked = masked_all[back - 1]
        ext[0:GROUP, :] = masked
        ext[GROUP : GROUP + 8, :] = edge[back - 1]
        draw = draw + cw_ref[3 - back : 4 - back, :] * ext[back : back + GROUP, :]
        edge[back - 1] = masked[0:8, :]
    gp_ref[:, hp : 2 * hp + 2 * STATE] = draw.astype(BF16)


def place_of(other, count):
    half = other >> 1
    if count == 8:
        half = half ^ (half >> 1)
    return half + (other & 1) * (count // 2)


def kernel_specs(hp, wid, n, reverse):
    def nat(i):
        return n - 1 - i if reverse else i

    def tok(i, base):
        return (place_of(nat(i) ^ base[0], n), 0)

    def prev(i, base):
        block = place_of(jnp.maximum(nat(i) - 1, 0) ^ base[0], n)
        return (block * (GROUP // 8) + GROUP // 8 - 1, 0)

    def same(i, base):
        return (0, 0)

    shared = [
        pl.BlockSpec((GROUP, wid), tok),
        pl.BlockSpec((8, wid), prev),
        pl.BlockSpec((GROUP, LANES), lambda i, base: (nat(i), 0)),
        pl.BlockSpec((8, GROUP), lambda i, base: (0, nat(i))),
        pl.BlockSpec((8, hp + 2 * STATE), same),
        pl.BlockSpec((8, LANES), same),
        pl.BlockSpec((8, hp), same),
        pl.BlockSpec((LANES, hp), same),
    ]
    state_spec = pl.BlockSpec((1, STATE, hp), lambda i, base: (nat(i), 0, 0))
    return tok, same, shared, state_spec


def ssd_forward(base, project, meta, segs, cw, dtp, chp, ex, *, hp, nh, cps):
    n = project.shape[0] // GROUP
    wid = project.shape[1]
    tok, _, shared, state_spec = kernel_specs(hp, wid, n, False)
    return pl.pallas_call(
        functools.partial(fwd_kernel, hp=hp, nh=nh, cps=cps),
        grid_spec=pltpu.PrefetchScalarGridSpec(
            num_scalar_prefetch=1,
            grid=(n,),
            in_specs=shared,
            out_specs=[
                pl.BlockSpec((GROUP, hp + LANES), tok),
                pl.BlockSpec((GROUP, hp), tok),
                state_spec,
            ],
            scratch_shapes=[
                pltpu.VMEM((STATE, hp), F32),
                pltpu.VMEM((GROUP + 8, hp + 2 * STATE), F32),
            ],
        ),
        out_shape=[
            jax.ShapeDtypeStruct((n * GROUP, hp + LANES), BF16),
            jax.ShapeDtypeStruct((n * GROUP, hp), F32),
            jax.ShapeDtypeStruct((n, STATE, hp), F32),
        ],
        cost_estimate=pl.CostEstimate(flops=10**9, bytes_accessed=4 * 10**7, transcendentals=0),
        name="ssd_forward",
    )(base, project, project, meta, segs, cw, dtp, chp, ex)


def ssd_backward(base, project, meta, segs, cw, dtp, chp, ex, y, states, gx, *, hp, nh, cps):
    n = project.shape[0] // GROUP
    wid = project.shape[1]
    tok, same, shared, state_spec = kernel_specs(hp, wid, n, True)
    wide = hp + 2 * STATE
    return pl.pallas_call(
        functools.partial(bwd_kernel, hp=hp, nh=nh, cps=cps),
        grid_spec=pltpu.PrefetchScalarGridSpec(
            num_scalar_prefetch=1,
            grid=(n,),
            in_specs=shared
            + [
                pl.BlockSpec((GROUP, hp), tok),
                state_spec,
                pl.BlockSpec((GROUP, hp + LANES), tok),
            ],
            out_specs=[
                pl.BlockSpec((GROUP, wid), tok),
                pl.BlockSpec((GROUP, hp), tok),
                pl.BlockSpec((8, wide), same),
                pl.BlockSpec((8, hp), same),
                pl.BlockSpec((8, LANES), same),
            ],
            scratch_shapes=[
                pltpu.VMEM((STATE, hp), F32),
                pltpu.VMEM((GROUP + 8, wide), F32),
                pltpu.VMEM((3, 8, wide), F32),
                pltpu.VMEM((LANES, GROUP), F32),
            ],
        ),
        out_shape=[
            jax.ShapeDtypeStruct((n * GROUP, wid), BF16),
            jax.ShapeDtypeStruct((n * GROUP, hp), BF16),
            jax.ShapeDtypeStruct((8, wide), F32),
            jax.ShapeDtypeStruct((8, hp), F32),
            jax.ShapeDtypeStruct((8, LANES), F32),
        ],
        cost_estimate=pl.CostEstimate(flops=10**9, bytes_accessed=8 * 10**7, transcendentals=0),
        name="ssd_backward",
    )(base, project, project, meta, segs, cw, dtp, chp, ex, y, states, gx)


def pad_to(a, axis, size):
    widths = [(0, 0)] * a.ndim
    widths[axis] = (0, size - a.shape[axis])
    return jnp.pad(a, widths)


def swap(a, axis, bit):
    size = lax.axis_size(axis)
    return lax.ppermute(a, axis, [(i, i ^ bit) for i in range(size)])


def far_first(count):
    return (6, 7, 2, 4, 3, 5, 1) if count == 8 else tuple(range(1, count))


def sum_all(a):
    for axis in ("fsdp", "cp"):
        bit = 1
        while bit < lax.axis_size(axis):
            a = a + swap(a, axis, bit)
            bit *= 2
    return a


def gather_plane(a, beside=()):
    fs = lax.axis_size("fsdp")
    if fs != 8:
        bit = 2
        while bit < fs:
            a = jnp.concatenate([a, swap(a, "fsdp", bit)], axis=0)
            bit *= 2
        return jnp.concatenate([a, swap(a, "fsdp", 1)], axis=0), beside
    half = a.shape[0] // 2
    along_x = swap(a, "fsdp", 2)
    along_y = swap(a, "fsdp", 4)
    mate = swap(a, "fsdp", 1)
    if beside:
        along_x, along_y, *beside = together(along_x, along_y, *beside)
    corner = jnp.concatenate(
        [swap(along_x[:half], "fsdp", 4), swap(along_y[half:], "fsdp", 2)], axis=0
    )
    mate_x = swap(along_x, "fsdp", 1)
    mate_y = swap(along_y, "fsdp", 1)
    mate_c = swap(corner, "fsdp", 1)
    parts = [a, along_x, corner, along_y, mate, mate_x, mate_c, mate_y]
    return jnp.concatenate(parts, axis=0), beside


def scatter_plane(rows, weight, contract, split, beside=(None, None)):
    fs = lax.axis_size("fsdp")
    half = rows.shape[0] // 2
    one, two = beside
    theirs = mm(rows[half:], weight, 1, contract).astype(BF16)
    mate = swap(theirs, "fsdp", 1)
    if one is not None:
        mate, one = together(mate, one)
    total = mm(rows[:half], weight, 1, contract) + mate.astype(F32)
    if fs != 8:
        bit = fs // 2
        while bit > 1:
            half = total.shape[0] // 2
            got = swap(total[half:].astype(BF16), "fsdp", bit)
            total = total[:half] + got.astype(F32)
            bit //= 2
        return total, one, two
    g = GROUP
    sent_x = swap(total[g : 3 * g, :split].astype(BF16), "fsdp", 2)
    sent_y = swap(total[2 * g :, split:].astype(BF16), "fsdp", 4)
    if two is not None:
        sent_x, sent_y, *two = together(sent_x, sent_y, *two)
    turn_y = (total[3 * g :, :split] + sent_x[g:].astype(F32)).astype(BF16)
    turn_x = (total[g : 2 * g, split:] + sent_y[:g].astype(F32)).astype(BF16)
    last_y = swap(turn_y, "fsdp", 4)
    last_x = swap(turn_x, "fsdp", 2)
    left = total[:g, :split] + sent_x[:g].astype(F32) + last_y.astype(F32)
    right = total[:g, split:] + sent_y[g:].astype(F32) + last_x.astype(F32)
    return jnp.concatenate([left, right], axis=1), one, two


def column_pieces(fs, cp):
    heads = HEADS // fs
    hc = heads * HEADDIM
    hp = (heads + heads % 2) * HEADDIM
    shard = PROJ // cp
    pieces = []
    for d in range(fs):
        mine = []
        for start, count, to in (
            (d * hc, hc, 0),
            (INNER + d * hc, hc, hp),
            (2 * INNER, 2 * STATE, 2 * hp),
            (INNER + CHANNELS + d * heads, heads, 2 * hp + 2 * STATE),
        ):
            while count:
                s, at = divmod(start, shard)
                n = min(count, shard - at)
                mine.append((s, at, n, to))
                start, count, to = start + n, count - n, to + n
        pieces.append(mine)
    return pieces


def pack_kernel(tie_ref, got_ref, out_ref, *, pieces):
    def some(k, _):
        rows = pl.ds(pl.multiple_of(k * ROWS, ROWS), ROWS)
        for d, mine in enumerate(pieces):
            out_ref[d, rows, :] = jnp.zeros_like(out_ref[d, rows, :])
            for s, at, n, to in mine:
                out_ref[d, rows, to : to + n] = got_ref[s, rows, at : at + n]
        return 0

    lax.fori_loop(0, got_ref.shape[1] // ROWS, some, 0)


def pack(tie, got, wid, fs, cp):
    return pl.pallas_call(
        functools.partial(pack_kernel, pieces=column_pieces(fs, cp)),
        in_specs=[
            pl.BlockSpec(memory_space=pltpu.SMEM),
            pl.BlockSpec(memory_space=pltpu.VMEM),
        ],
        out_shape=jax.ShapeDtypeStruct((fs, got.shape[1], wid), BF16),
        name="pack_columns",
    )(tie, got)


def unpack_kernel(f_ref, *refs, pieces, common, fs):
    blocks, out_ref, held, sems = refs[:fs], refs[fs], refs[fs + 1], refs[fs + 2]
    f = f_ref[0]
    copies = [
        pltpu.make_async_copy(blocks[r], held.at[f ^ r], sems.at[r]) for r in range(fs)
    ]
    for copy in copies:
        copy.start()
    for copy in copies:
        copy.wait()

    def some(k, _):
        rows = pl.ds(pl.multiple_of(k * ROWS, ROWS), ROWS)
        for d, mine in enumerate(pieces):
            for s, at, n, to in mine:
                if common[0] <= to < common[1]:
                    if d == 0:
                        both = held[0, rows, to : to + n].astype(F32)
                        for e in range(1, fs):
                            both = both + held[e, rows, to : to + n].astype(F32)
                        out_ref[s, rows, at : at + n] = both.astype(BF16)
                else:
                    out_ref[s, rows, at : at + n] = held[d, rows, to : to + n]
        return 0

    lax.fori_loop(0, out_ref.shape[1] // ROWS, some, 0)


def unpack(f, blocks, hp, fs, cp):
    rows, wid = blocks[0].shape
    return pl.pallas_call(
        functools.partial(
            unpack_kernel,
            pieces=column_pieces(fs, cp),
            common=(2 * hp, 2 * hp + 2 * STATE),
            fs=fs,
        ),
        in_specs=[pl.BlockSpec(memory_space=pltpu.SMEM)]
        + [pl.BlockSpec(memory_space=pl.ANY)] * fs,
        out_shape=jax.ShapeDtypeStruct((cp, rows, PROJ // cp), BF16),
        scratch_shapes=[pltpu.VMEM((fs, rows, wid), BF16), pltpu.SemaphoreType.DMA((fs,))],
        name="unpack_columns",
    )(f, *blocks)


def assemble_kernel(f_ref, packed, *refs, order):
    blocks, out_ref, sems = refs[: len(order)], refs[-2], refs[-1]
    f = f_ref[0]
    copies = [pltpu.make_async_copy(packed.at[f], out_ref.at[f], sems.at[0])]
    for k, r in enumerate(order):
        copies.append(pltpu.make_async_copy(blocks[k], out_ref.at[f ^ r], sems.at[k + 1]))
    for copy in copies:
        copy.start()
    for copy in copies:
        copy.wait()


def assemble(f, packed, blocks, order):
    return pl.pallas_call(
        functools.partial(assemble_kernel, order=order),
        in_specs=[pl.BlockSpec(memory_space=pltpu.SMEM)]
        + [pl.BlockSpec(memory_space=pl.ANY)] * (1 + len(blocks)),
        out_specs=pl.BlockSpec(memory_space=pltpu.VMEM),
        out_shape=jax.ShapeDtypeStruct(packed.shape, packed.dtype),
        scratch_shapes=[pltpu.SemaphoreType.DMA((1 + len(blocks),))],
        name="assemble_rows",
    )(f, packed, *blocks)


def together(*values):
    return lax.optimization_barrier(values)


def scale_of(u):
    return lax.rsqrt(jnp.mean(u * u, axis=-1, keepdims=True) + EPSILON)


def split_two(v):
    high = lax.reduce_precision(v, 8, 7)
    return high.astype(BF16), (v - high).astype(BF16)


def steps(
    hidden, d_out, seg_ids, w_in, w_out, norm_in, norm_gate, conv_w, conv_b, dt_bias, a_log, d_skip
):
    fs, cp = lax.axis_size("fsdp"), lax.axis_size("cp")
    f = lax.axis_index("fsdp")
    width = hidden.shape[-1]
    heads = HEADS // fs
    nh = heads + heads % 2
    hc, hp = heads * HEADDIM, nh * HEADDIM
    wid = 2 * hp + 2 * STATE + LANES
    rows_in = width // fs
    cps = cp
    per = fs // cp
    planes = [k // 2 if k % 2 == 0 else cp - 1 - k // 2 for k in range(cp)]
    there = [
        (a * cp + b, ((a // cp) * cp + b) * cp + planes[a % cp])
        for a in range(fs)
        for b in range(cp)
    ]
    back = [(b, a) for a, b in there]
    base = f.astype(jnp.int32).reshape(1)

    def move(a, route):
        return lax.ppermute(a, ("fsdp", "cp"), route)

    first = hidden.reshape(GROUP, width)
    scale = scale_of(first)
    normed = lax.reduce_precision(first * scale * norm_in[0], 8, 7)
    high, low = split_two(1.0 / scale)

    def rebuilt(normed, high, low):
        return normed.astype(F32) * (high.astype(F32) + low.astype(F32)) / norm_in[0]

    left_over = (first - rebuilt(normed, high, low)).astype(BF16)
    normed = normed.astype(BF16)
    marks = pad_to(
        jnp.concatenate([seg_ids.reshape(GROUP, 1).astype(BF16), high, low], axis=1), 1, LANES
    )
    moved = move(jnp.concatenate([normed, marks], axis=1), there)
    left_over = move(left_over, there)
    own_scale = moved[:, width + 1 : width + 3]
    own_normed = moved[:, :width]
    marked, _ = gather_plane(moved)
    normed_all = marked[:, :width]
    marks = marked[:, width].astype(F32).reshape(fs, GROUP)
    natural = [place_of(jnp.asarray(k) ^ f, fs) for k in range(fs)]
    segs = jnp.stack(
        [lax.dynamic_index_in_dim(marks, n, 0, False) for n in natural]
    ).reshape(per, cps * GROUP)
    total = per * cps * GROUP
    place = jnp.arange(cps * GROUP)
    cols = []
    for k in (1, 2, 3):
        before = jnp.roll(segs, k, axis=1)
        cols.append(jnp.logical_and(before == segs, place[None, :] >= k).astype(F32))
    grouped = segs.reshape(per, cps, GROUP)
    before = jnp.concatenate([segs[:, :1], grouped[:, :-1, -1]], axis=1)
    keep = (grouped == before[:, :, None]).astype(F32)
    tail = (grouped == grouped[:, :, -1:]).astype(F32)
    cols += [keep, tail, grouped, jnp.broadcast_to(keep[:, :, -1:], keep.shape)]
    meta = pad_to(jnp.stack([c.reshape(total) for c in cols], axis=1), 1, LANES)
    seg_rows = jnp.broadcast_to(segs.reshape(1, total), (8, total))
    ex = (jnp.arange(hp)[None, :] // HEADDIM == jnp.arange(LANES)[:, None]).astype(BF16)

    eye = jnp.eye(LANES, dtype=BF16)

    def send_in(packed):
        return [
            swap(lax.dynamic_index_in_dim(packed, f ^ r, 0, False), "fsdp", r)
            for r in far_first(fs)
        ]

    def place_in(packed, blocks):
        return assemble(base, packed, blocks, far_first(fs)).reshape(width, wid)

    def finish_out(got):
        out_w = pad_to(got.transpose(1, 0, 2).reshape(hc, width), 0, hp)
        return jnp.concatenate(
            [
                pad_to(out_w, 1, width + LANES),
                jnp.concatenate([jnp.zeros((LANES, width), BF16), eye], axis=1),
            ],
            axis=0,
        )

    def gather_cp(a):
        return lax.all_gather(a, "cp", axis=0)

    got_in, got_out = [None] * LAYERS, [None] * LAYERS
    got_in[0] = gather_cp(w_in[0])
    last_grad = d_out.reshape(GROUP, width)
    packed = pack(jnp.zeros((1,), F32), got_in[0], wid, fs, cp)
    full_in, full_out = [place_in(packed, send_in(packed))], []
    for i in range(LAYERS):
        if i:
            got_in[i] = gather_cp(w_in[i])
        got_out[i] = gather_cp(w_out[i])

    def own(v, size, padded):
        return pad_to(lax.dynamic_slice_in_dim(v, f * size, size, v.ndim - 1), v.ndim - 1, padded)

    params = []
    for i in range(LAYERS):
        taps = jnp.concatenate([conv_w[i], conv_b[i][None]], axis=0)
        cw = jnp.concatenate([own(taps[:, :INNER], hc, hp), taps[:, INNER:]], axis=1)
        rate = -jnp.exp(own(a_log[i], heads, heads))
        dtp = jnp.stack([own(dt_bias[i], heads, LANES), pad_to(rate, 0, LANES)])
        skip = own(jnp.repeat(d_skip[i], HEADDIM), hc, hp)
        chp = jnp.stack([skip, own(norm_gate[i], hc, hp)])
        params.append((pad_to(cw, 0, 8), pad_to(dtp, 0, 8), pad_to(chp, 0, 8), ex))

    saved = []
    sizes = dict(hp=hp, nh=nh, cps=cps)
    added = 0.0
    for i in range(LAYERS):
        if i:
            normed = (current * scale_of(current) * norm_in[i]).astype(BF16)
            normed_all, blocks = gather_plane(normed, blocks)
            full_in.append(place_in(packed, blocks))
        project = mm(normed_all, full_in[i], 1, 0)
        if i + 1 < LAYERS:
            packed = pack(project[0, :1], got_in[i + 1], wid, fs, cp)
            project, packed = together(project, packed)
            blocks = send_in(packed)
        if i + 1 == LAYERS:
            project, last_grad = together(project, last_grad)
            moved_grad = move(last_grad.astype(BF16), there)
        rg, y, states = ssd_forward(base, project, meta, seg_rows, *params[i], **sizes)
        rg, got_out[i] = together(rg, got_out[i])
        full_out.append(finish_out(got_out[i]))
        summed, _, _ = scatter_plane(rg, full_out[i], 0, width // 2)
        inv = lax.rsqrt(
            jnp.sum(summed[:, width:], axis=1, keepdims=True) * (1.0 / INNER) + EPSILON
        )
        branch = summed[:, :width] * inv
        if i == 0:
            current = rebuilt(own_normed, own_scale[:, :1], own_scale[:, 1:]) + left_over
        saved.append((current, normed_all, project, y, states, branch, inv))
        current = current + branch
        added = added + branch
    activations = first + move(added.astype(BF16), back).astype(F32)

    grads_in, grads_out, small = [None] * LAYERS, [None] * LAYERS, [None] * LAYERS
    change = 0.0
    waiting = None

    def send_out(d_wi):
        blocks = {0: lax.dynamic_index_in_dim(d_wi, f, 0, False)}
        for r in far_first(fs):
            blocks[r] = swap(lax.dynamic_index_in_dim(d_wi, f ^ r, 0, False), "fsdp", r)
        return [blocks[r] for r in range(fs)]

    def sum_in(wide):
        wide = lax.psum_scatter(wide, "cp", scatter_dimension=0, tiled=True)
        return wide[0].astype(F32)

    for i in reversed(range(LAYERS)):
        before, normed_all, project, y, states, branch, inv = saved[i]
        grad_b = (moved_grad.astype(F32) + change).astype(BF16)
        dots = jnp.sum(branch * grad_b.astype(F32), axis=1, keepdims=True)
        scal = jnp.concatenate([*split_two(inv), *split_two(dots)], axis=1)
        payload = jnp.concatenate([grad_b, pad_to(scal, 1, LANES)], axis=1)
        if waiting is not None:
            payload, waiting = gather_plane(payload, waiting)
            wide = unpack(base, send_out(waiting[0]), hp, fs, cp)
        else:
            payload, _ = gather_plane(payload)
        gx = mm(payload, full_out[i], 1, 1)
        gp, gated, gcw, gch, gdt = ssd_backward(
            base, project, meta, seg_rows, *params[i], y, states, gx, **sizes
        )
        if waiting is not None:
            gp, wide, grads_out[i + 1] = together(gp, wide, grads_out[i + 1])
            grads_in[i + 1] = sum_in(wide)
        d_wi = mm(normed_all, gp, 0, 0).astype(BF16).reshape(fs, rows_in, wid)
        d_wo = mm(gated[:, :hc], payload[:, :width], 0, 0).astype(BF16)
        if i:
            g_normed, d_wo, waiting = scatter_plane(
                gp, full_in[i], 1, width // 2, (d_wo, [d_wi])
            )
        else:
            gp, d_wi, d_wo = together(gp, d_wi, d_wo)
            blocks = send_out(d_wi)
            g_normed, _, blocks = scatter_plane(gp, full_in[i], 1, width // 2, (None, blocks))
        d_wo = d_wo.reshape(hc, cp, width // cp).transpose(1, 0, 2)
        d_wo = lax.psum_scatter(d_wo, "cp", scatter_dimension=0, tiled=True)
        grads_out[i] = d_wo[0].astype(F32)
        if i == 0:
            wide = unpack(base, blocks, hp, fs, cp)
            wide, grads_in[i + 1] = together(wide, grads_in[i + 1])
            grads_in[i] = sum_in(wide)

        scale = scale_of(before)
        hat = before * scale
        pulled = g_normed * norm_in[i]
        change = change + scale * (pulled - hat * jnp.mean(pulled * hat, axis=-1, keepdims=True))
        g_norm_in = jnp.sum(g_normed * hat, axis=0)

        table = jnp.zeros((8, CHANNELS), F32)
        mine = jnp.concatenate([gcw[:5, :hc], gch[1:2, :hc]], axis=0)
        table = lax.dynamic_update_slice(table, mine, (0, f * hc))
        table = table.at[:5, INNER:].add(gcw[:5, hp:])
        table = table.at[6, :width].set(g_norm_in)
        by_head = jnp.sum(gch[0, :hc].reshape(heads, HEADDIM), axis=1)
        rate = -jnp.exp(own(a_log[i], heads, heads))
        thin = jnp.stack([gdt[0, :heads], gdt[1, :heads] * rate, by_head])
        thin = lax.dynamic_update_slice(jnp.zeros((3, HEADS), F32), thin, (0, f * heads))
        table = table.at[7, : 3 * HEADS].set(thin.reshape(-1))
        small[i] = table

    d_hidden = last_grad + move(change.astype(BF16), back).astype(F32)
    tables = sum_all(jnp.stack(small))
    shape = hidden.shape
    thin = tables[:, 7, : 3 * HEADS].reshape(LAYERS, 3, HEADS)
    return (
        activations.reshape(shape),
        d_hidden.reshape(shape),
        jnp.stack(grads_in),
        jnp.stack(grads_out),
        tables[:, 6, :width],
        tables[:, 5, :INNER],
        tables[:, :4],
        tables[:, 4],
        thin[:, 0],
        thin[:, 1],
        thin[:, 2],
    )


def solution(mesh):
    in_specs = (
        P("fsdp", "cp", None),
        P("fsdp", "cp", None),
        P("fsdp", "cp"),
        P(None, "fsdp", "cp"),
        P(None, "fsdp", "cp"),
    ) + (P(),) * 7
    out_specs = (
        P("fsdp", "cp", None),
        P("fsdp", "cp", None),
        P(None, "fsdp", "cp"),
        P(None, "fsdp", "cp"),
    ) + (P(),) * 7
    return jax.shard_map(steps, mesh=mesh, in_specs=in_specs, out_specs=out_specs, check_vma=False)
```

```python
import functools

import jax
import jax.numpy as jnp
from jax import lax
from jax.experimental import pallas as pl
from jax.experimental.pallas import tpu as pltpu
from jax.sharding import PartitionSpec as P


HEADS = 48
HEADDIM = 64
STATE = 128
LAYERS = 2
INNER = 3072
CHANNELS = 3328
PROJ = 6448
GROUP = 128
EPSILON = 1e-05
LANES = 128
ROWS = 32

F32 = jnp.float32
BF16 = jnp.bfloat16


def mm(a, b, ca, cb, precision=None):
    return lax.dot_general(
        a, b, (((ca,), (cb,)), ((), ())), precision=precision, preferred_element_type=F32
    )


def parts_of(v):
    high = v.astype(BF16)
    return high, (v - high.astype(F32)).astype(BF16)


def fine(a, b, ca, cb):
    return mm(a[0], b[0], ca, cb) + (mm(a[0], b[1], ca, cb) + mm(a[1], b[0], ca, cb))


def by_mask(v, ex, cb):
    high, low = parts_of(v)
    return mm(high, ex, 1, cb) + mm(low, ex, 1, cb)


def summed_rows(tri, v, ca):
    high = v.astype(BF16)
    rest = v - high.astype(F32)
    middle = rest.astype(BF16)
    low = (rest - middle.astype(F32)).astype(BF16)
    return mm(tri, high, ca, 0) + (mm(tri, middle, ca, 0) + mm(tri, low, ca, 0))


def sigmoid(v):
    return 1.0 / (1.0 + jnp.exp(-v))


def conv_parts(p_ref, prev_ref, ext, meta, cw_ref, hp):
    wide = hp + 2 * STATE
    raw = p_ref[:, hp : hp + wide]
    ext[0:8, :] = prev_ref[:, hp : hp + wide]
    ext[8 : 8 + GROUP, :] = raw
    pre = cw_ref[4:5, :] + cw_ref[3:4, :] * raw
    taps = [raw]
    for back in (1, 2, 3):
        shifted = ext[8 - back : 8 - back + GROUP, :]
        taps.append(shifted)
        pre = pre + cw_ref[3 - back : 4 - back, :] * shifted * meta[:, back - 1 : back]
    return pre, taps


def decay_parts(p_ref, meta, dtp_ref, hp):
    u = p_ref[:, 2 * hp + 2 * STATE :] + dtp_ref[0:1, :]
    dt = jnp.maximum(u, 0.0) + jnp.log1p(jnp.exp(-jnp.abs(u)))
    rows = lax.broadcasted_iota(jnp.int32, (GROUP, GROUP), 0)
    cols = lax.broadcasted_iota(jnp.int32, (GROUP, GROUP), 1)
    lower = rows >= cols
    tri = lower.astype(F32).astype(BF16)
    cum = summed_rows(tri, dt * dtp_ref[1:2, :], 1)
    last = cum[GROUP - 1 : GROUP, :]
    into = jnp.exp(cum) * meta[:, 3:4]
    tail = jnp.exp(last - cum) * meta[:, 4:5]
    through = jnp.exp(last) * meta[0:1, 6:7]
    return u, dt, cum, into, tail, through, lower, tri, rows


def fwd_kernel(
    base_ref, p_ref, prev_ref, meta_ref, seg_ref, cw_ref, dtp_ref, chp_ref, ex_ref,
    rg_ref, y_ref, st_ref, state, ext, *, hp, nh, cps,
):
    j = pl.program_id(0)

    @pl.when(lax.rem(j, cps) == 0)
    def _():
        state[...] = jnp.zeros_like(state)

    meta = meta_ref[...]
    pre, _ = conv_parts(p_ref, prev_ref, ext, meta, cw_ref, hp)
    mixed = pre * sigmoid(pre)
    x = mixed[:, :hp]
    b_rows = parts_of(mixed[:, hp : hp + STATE])
    c_rows = parts_of(mixed[:, hp + STATE :])
    _, dt, cum, into, tail, through, lower, _, _ = decay_parts(p_ref, meta, dtp_ref, hp)
    cum_t = cum.T
    dt_t = dt.T
    scores = fine(c_rows, b_rows, 1, 1)
    same = jnp.logical_and(lower, meta[:, 5:6] == seg_ref[0:1, :])
    ex = ex_ref[...]
    into_x = by_mask(into, ex, 0)
    weight_x = by_mask(tail * dt, ex, 0)
    through_x = by_mask(jnp.broadcast_to(through, (8, LANES)), ex, 0)[0:1, :]
    old = state[...]
    st_ref[0] = old
    carried = fine(c_rows, parts_of(old), 1, 0) * into_x
    state[...] = old * through_x + fine(b_rows, parts_of(x * weight_x), 0, 0)
    low_half = lax.broadcasted_iota(jnp.int32, (GROUP, LANES), 1) < HEADDIM
    total = jnp.zeros((GROUP, LANES), F32)
    for pair in range(nh // 2):
        at = slice(pair * LANES, (pair + 1) * LANES)
        xp = x[:, at]
        xb = parts_of(xp)
        halves = []
        for h in (2 * pair, 2 * pair + 1):
            spread = cum[:, h : h + 1] - cum_t[h : h + 1, :]
            mixing = scores * jnp.exp(jnp.where(same, spread, -1e30)) * dt_t[h : h + 1, :]
            halves.append(fine(parts_of(mixing), xb, 1, 0))
        y = jnp.where(low_half, halves[0], halves[1]) + carried[:, at] + chp_ref[0:1, at] * xp
        y_ref[:, at] = y
        z = p_ref[:, at]
        r = y * (z * sigmoid(z))
        rg_ref[:, at] = (r * chp_ref[1:2, at]).astype(BF16)
        total = total + r * r
    rg_ref[:, hp:] = total.astype(BF16)


def bwd_kernel(
    base_ref, p_ref, prev_ref, meta_ref, seg_ref, cw_ref, dtp_ref, chp_ref, ex_ref,
    y_ref, st_ref, gx_ref,
    gp_ref, gated_ref, gcw_ref, gch_ref, gdt_ref,
    dstate, ext, edge, row_sums, *, hp, nh, cps,
):
    step = pl.program_id(0)
    j = pl.num_programs(0) - 1 - step

    @pl.when(step == 0)
    def _():
        gcw_ref[...] = jnp.zeros_like(gcw_ref)
        gch_ref[...] = jnp.zeros_like(gch_ref)
        gdt_ref[...] = jnp.zeros_like(gdt_ref)
        row_sums[...] = jnp.zeros_like(row_sums)

    @pl.when(lax.rem(j, cps) == cps - 1)
    def _():
        dstate[...] = jnp.zeros_like(dstate)
        edge[...] = jnp.zeros_like(edge)

    meta = meta_ref[...]
    pre, taps = conv_parts(p_ref, prev_ref, ext, meta, cw_ref, hp)
    sig = sigmoid(pre)
    mixed = pre * sig
    x = mixed[:, :hp]
    b_rows = parts_of(mixed[:, hp : hp + STATE])
    c_rows = parts_of(mixed[:, hp + STATE :])
    u, dt, cum, into, tail, through, lower, tri, rows = decay_parts(p_ref, meta, dtp_ref, hp)
    cum_t = cum.T
    dt_t = dt.T
    scores = fine(c_rows, b_rows, 1, 1)
    same = jnp.logical_and(lower, meta[:, 5:6] == seg_ref[0:1, :])
    ex = ex_ref[...]
    weight = tail * dt
    into_x = by_mask(into, ex, 0)
    weight_x = by_mask(weight, ex, 0)
    through_x = by_mask(jnp.broadcast_to(through, (8, LANES)), ex, 0)[0:1, :]

    scal = gx_ref[:, hp:]
    inv = scal[:, 0:1] + scal[:, 1:2]
    pull = (scal[:, 2:3] + scal[:, 3:4]) * inv * inv * (1.0 / INNER)
    low_half = lax.broadcasted_iota(jnp.int32, (GROUP, LANES), 1) < HEADDIM
    lane = lax.broadcasted_iota(jnp.int32, (GROUP, LANES), 1)
    dys = []
    for pair in range(nh // 2):
        at = slice(pair * LANES, (pair + 1) * LANES)
        z, y, g = p_ref[:, at], y_ref[:, at], gx_ref[:, at]
        gain = chp_ref[1:2, at]
        sz = sigmoid(z)
        silu = z * sz
        r = y * silu
        scaled = r * inv
        gated_ref[:, at] = (scaled * gain).astype(BF16)
        gch_ref[1:2, at] += jnp.sum(g * scaled, axis=0, keepdims=True)
        dr = inv * (g * gain) - r * pull
        dys.append(dr * silu)
        gp_ref[:, at] = (dr * y * (sz * (1.0 + z * (1.0 - sz)))).astype(BF16)
    dy = jnp.concatenate(dys, axis=1)

    old = st_ref[0]
    after = dstate[...]
    old_b, after_b = parts_of(old), parts_of(after)
    dxw = fine(b_rows, after_b, 1, 0)
    dx_wide = dxw * weight_x + chp_ref[0:1, :] * dy
    db = fine(parts_of(x * weight_x), after_b, 1, 1)
    dye = parts_of(dy * into_x)
    dc = fine(dye, old_b, 1, 1)
    dweight = by_mask(dxw * x, ex, 1)
    dinto = by_mask(dy * fine(c_rows, old_b, 1, 0), ex, 1)
    dthrough = by_mask(
        jnp.broadcast_to(jnp.sum(old * after, axis=0, keepdims=True), (8, hp)), ex, 1
    )[0:1, :]
    dstate[...] = after * through_x + fine(c_rows, dye, 0, 0)
    gch_ref[0:1, :] += jnp.sum(dy * x, axis=0, keepdims=True)

    dscores = jnp.zeros((GROUP, GROUP), F32)
    row_part = jnp.zeros((GROUP, LANES), F32)
    dx_parts = []
    for pair in range(nh // 2):
        at = slice(pair * LANES, (pair + 1) * LANES)
        xb = parts_of(x[:, at])
        dyb = parts_of(dy[:, at])
        halves = []
        for side in (0, 1):
            h = 2 * pair + side
            mine = low_half if side == 0 else jnp.logical_not(low_half)
            spread = cum[:, h : h + 1] - cum_t[h : h + 1, :]
            decay = jnp.exp(jnp.where(same, spread, -1e30))
            dtr = dt_t[h : h + 1, :]
            decayed = scores * decay
            mixing = parts_of(decayed * dtr)
            dmix = fine([jnp.where(mine, v, jnp.zeros_like(v)) for v in dyb], xb, 1, 1)
            dscores = dscores + dmix * decay * dtr
            flow = dmix * decayed
            row_sums[h : h + 1, :] = jnp.sum(flow, axis=0, keepdims=True)
            across = jnp.sum(flow * dtr, axis=1, keepdims=True)
            row_part = jnp.where(lane == h, across, row_part)
            halves.append(fine(mixing, dyb, 0, 0))
        dx_parts.append(jnp.where(low_half, halves[0], halves[1]))
    dx_wide = dx_wide + jnp.concatenate(dx_parts, axis=1)
    dsb = parts_of(dscores)
    db = db + fine(dsb, c_rows, 0, 0)
    dc = dc + fine(dsb, b_rows, 1, 0)

    col_part = row_sums[...].T
    used = dweight * weight
    at_last = jnp.sum(used, axis=0, keepdims=True) + dthrough * through
    dcum = row_part + dinto * into - dt * col_part - used
    dcum = dcum + jnp.where(rows == GROUP - 1, at_last, 0.0)
    dstep = summed_rows(tri, dcum, 0)
    ddt = col_part + dweight * tail + dstep * dtp_ref[1:2, :]
    du = ddt * sigmoid(u)
    gdt_ref[0:1, :] += jnp.sum(du, axis=0, keepdims=True)
    gdt_ref[1:2, :] += jnp.sum(dstep * dt, axis=0, keepdims=True)
    gp_ref[:, 2 * hp + 2 * STATE :] = du.astype(BF16)

    dmixed = jnp.concatenate([dx_wide, db, dc], axis=1)
    dpre = dmixed * (sig * (1.0 + pre * (1.0 - sig)))
    gcw_ref[4:5, :] += jnp.sum(dpre, axis=0, keepdims=True)
    gcw_ref[3:4, :] += jnp.sum(dpre * taps[0], axis=0, keepdims=True)
    draw = cw_ref[3:4, :] * dpre
    masked_all = []
    for back in (1, 2, 3):
        masked = dpre * meta[:, back - 1 : back]
        gcw_ref[3 - back : 4 - back, :] += jnp.sum(masked * taps[back], axis=0, keepdims=True)
        masked_all.append(masked)
    for back in (1, 2, 3):
        masked = masked_all[back - 1]
        ext[0:GROUP, :] = masked
        ext[GROUP : GROUP + 8, :] = edge[back - 1]
        draw = draw + cw_ref[3 - back : 4 - back, :] * ext[back : back + GROUP, :]
        edge[back - 1] = masked[0:8, :]
    gp_ref[:, hp : 2 * hp + 2 * STATE] = draw.astype(BF16)


def place_of(other, count):
    half = other >> 1
    if count == 8:
        half = half ^ (half >> 1)
    return half + (other & 1) * (count // 2)


def kernel_specs(hp, wid, n, reverse):
    def nat(i):
        return n - 1 - i if reverse else i

    def tok(i, base):
        return (place_of(nat(i) ^ base[0], n), 0)

    def prev(i, base):
        block = place_of(jnp.maximum(nat(i) - 1, 0) ^ base[0], n)
        return (block * (GROUP // 8) + GROUP // 8 - 1, 0)

    def same(i, base):
        return (0, 0)

    shared = [
        pl.BlockSpec((GROUP, wid), tok),
        pl.BlockSpec((8, wid), prev),
        pl.BlockSpec((GROUP, LANES), lambda i, base: (nat(i), 0)),
        pl.BlockSpec((8, GROUP), lambda i, base: (0, nat(i))),
        pl.BlockSpec((8, hp + 2 * STATE), same),
        pl.BlockSpec((8, LANES), same),
        pl.BlockSpec((8, hp), same),
        pl.BlockSpec((LANES, hp), same),
    ]
    state_spec = pl.BlockSpec((1, STATE, hp), lambda i, base: (nat(i), 0, 0))
    return tok, same, shared, state_spec


def ssd_forward(base, project, meta, segs, cw, dtp, chp, ex, *, hp, nh, cps):
    n = project.shape[0] // GROUP
    wid = project.shape[1]
    tok, _, shared, state_spec = kernel_specs(hp, wid, n, False)
    return pl.pallas_call(
        functools.partial(fwd_kernel, hp=hp, nh=nh, cps=cps),
        grid_spec=pltpu.PrefetchScalarGridSpec(
            num_scalar_prefetch=1,
            grid=(n,),
            in_specs=shared,
            out_specs=[
                pl.BlockSpec((GROUP, hp + LANES), tok),
                pl.BlockSpec((GROUP, hp), tok),
                state_spec,
            ],
            scratch_shapes=[
                pltpu.VMEM((STATE, hp), F32),
                pltpu.VMEM((GROUP + 8, hp + 2 * STATE), F32),
            ],
        ),
        out_shape=[
            jax.ShapeDtypeStruct((n * GROUP, hp + LANES), BF16),
            jax.ShapeDtypeStruct((n * GROUP, hp), F32),
            jax.ShapeDtypeStruct((n, STATE, hp), F32),
        ],
        cost_estimate=pl.CostEstimate(flops=10**9, bytes_accessed=4 * 10**7, transcendentals=0),
        name="ssd_forward",
    )(base, project, project, meta, segs, cw, dtp, chp, ex)


def ssd_backward(base, project, meta, segs, cw, dtp, chp, ex, y, states, gx, *, hp, nh, cps):
    n = project.shape[0] // GROUP
    wid = project.shape[1]
    tok, same, shared, state_spec = kernel_specs(hp, wid, n, True)
    wide = hp + 2 * STATE
    return pl.pallas_call(
        functools.partial(bwd_kernel, hp=hp, nh=nh, cps=cps),
        grid_spec=pltpu.PrefetchScalarGridSpec(
            num_scalar_prefetch=1,
            grid=(n,),
            in_specs=shared
            + [
                pl.BlockSpec((GROUP, hp), tok),
                state_spec,
                pl.BlockSpec((GROUP, hp + LANES), tok),
            ],
            out_specs=[
                pl.BlockSpec((GROUP, wid), tok),
                pl.BlockSpec((GROUP, hp), tok),
                pl.BlockSpec((8, wide), same),
                pl.BlockSpec((8, hp), same),
                pl.BlockSpec((8, LANES), same),
            ],
            scratch_shapes=[
                pltpu.VMEM((STATE, hp), F32),
                pltpu.VMEM((GROUP + 8, wide), F32),
                pltpu.VMEM((3, 8, wide), F32),
                pltpu.VMEM((LANES, GROUP), F32),
            ],
        ),
        out_shape=[
            jax.ShapeDtypeStruct((n * GROUP, wid), BF16),
            jax.ShapeDtypeStruct((n * GROUP, hp), BF16),
            jax.ShapeDtypeStruct((8, wide), F32),
            jax.ShapeDtypeStruct((8, hp), F32),
            jax.ShapeDtypeStruct((8, LANES), F32),
        ],
        cost_estimate=pl.CostEstimate(flops=10**9, bytes_accessed=8 * 10**7, transcendentals=0),
        name="ssd_backward",
    )(base, project, project, meta, segs, cw, dtp, chp, ex, y, states, gx)


def pad_to(a, axis, size):
    widths = [(0, 0)] * a.ndim
    widths[axis] = (0, size - a.shape[axis])
    return jnp.pad(a, widths)


def swap(a, axis, bit):
    size = lax.axis_size(axis)
    return lax.ppermute(a, axis, [(i, i ^ bit) for i in range(size)])


def far_first(count):
    return (6, 7, 2, 4, 3, 5, 1) if count == 8 else tuple(range(1, count))


def sum_over(axis, a):
    bit = 1
    while bit < lax.axis_size(axis):
        a = a + swap(a, axis, bit)
        bit *= 2
    return a


def gather_plane(a, beside=()):
    fs = lax.axis_size("fsdp")
    if fs != 8:
        bit = 2
        while bit < fs:
            a = jnp.concatenate([a, swap(a, "fsdp", bit)], axis=0)
            bit *= 2
        return jnp.concatenate([a, swap(a, "fsdp", 1)], axis=0), beside
    half = a.shape[0] // 2
    along_x = swap(a, "fsdp", 2)
    along_y = swap(a, "fsdp", 4)
    mate = swap(a, "fsdp", 1)
    if beside:
        along_x, along_y, *beside = together(along_x, along_y, *beside)
    corner = jnp.concatenate(
        [swap(along_x[:half], "fsdp", 4), swap(along_y[half:], "fsdp", 2)], axis=0
    )
    mate_x = swap(along_x, "fsdp", 1)
    mate_y = swap(along_y, "fsdp", 1)
    mate_c = swap(corner, "fsdp", 1)
    parts = [a, along_x, corner, along_y, mate, mate_x, mate_c, mate_y]
    return jnp.concatenate(parts, axis=0), beside


def scatter_plane(rows, weight, contract, split, beside=(None, None), hold=()):
    fs = lax.axis_size("fsdp")
    half = rows.shape[0] // 2
    one, two = beside
    theirs = mm(rows[half:], weight, 1, contract).astype(BF16)
    mate = swap(theirs, "fsdp", 1)
    if one is not None:
        mate, one = together(mate, one)
    total = mm(rows[:half], weight, 1, contract) + mate.astype(F32)
    if hold:
        total, *hold = together(total, *hold)
    if fs != 8:
        bit = fs // 2
        while bit > 1:
            half = total.shape[0] // 2
            got = swap(total[half:].astype(BF16), "fsdp", bit)
            total = total[:half] + got.astype(F32)
            bit //= 2
        return total, one, two, hold
    g = GROUP
    sent_x = swap(total[g : 3 * g, :split].astype(BF16), "fsdp", 2)
    sent_y = swap(total[2 * g :, split:].astype(BF16), "fsdp", 4)
    if two is not None:
        sent_x, sent_y, *two = together(sent_x, sent_y, *two)
    turn_y = (total[3 * g :, :split] + sent_x[g:].astype(F32)).astype(BF16)
    turn_x = (total[g : 2 * g, split:] + sent_y[:g].astype(F32)).astype(BF16)
    last_y = swap(turn_y, "fsdp", 4)
    last_x = swap(turn_x, "fsdp", 2)
    left = total[:g, :split] + sent_x[:g].astype(F32) + last_y.astype(F32)
    right = total[:g, split:] + sent_y[g:].astype(F32) + last_x.astype(F32)
    return jnp.concatenate([left, right], axis=1), one, two, hold


def column_pieces(fs, cp):
    heads = HEADS // fs
    hc = heads * HEADDIM
    hp = (heads + heads % 2) * HEADDIM
    shard = PROJ // cp
    pieces = []
    for d in range(fs):
        mine = []
        for start, count, to in (
            (d * hc, hc, 0),
            (INNER + d * hc, hc, hp),
            (2 * INNER, 2 * STATE, 2 * hp),
            (INNER + CHANNELS + d * heads, heads, 2 * hp + 2 * STATE),
        ):
            while count:
                s, at = divmod(start, shard)
                n = min(count, shard - at)
                mine.append((s, at, n, to))
                start, count, to = start + n, count - n, to + n
        pieces.append(mine)
    return pieces


def pack_kernel(tie_ref, got_ref, out_ref, *, pieces):
    def some(k, _):
        rows = pl.ds(pl.multiple_of(k * ROWS, ROWS), ROWS)
        for d, mine in enumerate(pieces):
            out_ref[d, rows, :] = jnp.zeros_like(out_ref[d, rows, :])
            for s, at, n, to in mine:
                out_ref[d, rows, to : to + n] = got_ref[s, rows, at : at + n]
        return 0

    lax.fori_loop(0, got_ref.shape[1] // ROWS, some, 0)


def pack(tie, got, wid, fs, cp):
    return pl.pallas_call(
        functools.partial(pack_kernel, pieces=column_pieces(fs, cp)),
        in_specs=[
            pl.BlockSpec(memory_space=pltpu.SMEM),
            pl.BlockSpec(memory_space=pltpu.VMEM),
        ],
        out_shape=jax.ShapeDtypeStruct((fs, got.shape[1], wid), BF16),
        name="pack_columns",
    )(tie, got)


def unpack_kernel(f_ref, *refs, pieces, common, fs):
    blocks, out_ref, held, sems = refs[:fs], refs[fs], refs[fs + 1], refs[fs + 2]
    f = f_ref[0]
    copies = [
        pltpu.make_async_copy(blocks[r], held.at[f ^ r], sems.at[r]) for r in range(fs)
    ]
    for copy in copies:
        copy.start()
    for copy in copies:
        copy.wait()

    def some(k, _):
        rows = pl.ds(pl.multiple_of(k * ROWS, ROWS), ROWS)
        for d, mine in enumerate(pieces):
            for s, at, n, to in mine:
                if common[0] <= to < common[1]:
                    if d == 0:
                        both = held[0, rows, to : to + n].astype(F32)
                        for e in range(1, fs):
                            both = both + held[e, rows, to : to + n].astype(F32)
                        out_ref[s, rows, at : at + n] = both.astype(BF16)
                else:
                    out_ref[s, rows, at : at + n] = held[d, rows, to : to + n]
        return 0

    lax.fori_loop(0, out_ref.shape[1] // ROWS, some, 0)


def unpack(f, blocks, hp, fs, cp):
    rows, wid = blocks[0].shape
    return pl.pallas_call(
        functools.partial(
            unpack_kernel,
            pieces=column_pieces(fs, cp),
            common=(2 * hp, 2 * hp + 2 * STATE),
            fs=fs,
        ),
        in_specs=[pl.BlockSpec(memory_space=pltpu.SMEM)]
        + [pl.BlockSpec(memory_space=pl.ANY)] * fs,
        out_shape=jax.ShapeDtypeStruct((cp, rows, PROJ // cp), BF16),
        scratch_shapes=[pltpu.VMEM((fs, rows, wid), BF16), pltpu.SemaphoreType.DMA((fs,))],
        name="unpack_columns",
    )(f, *blocks)


def assemble_kernel(f_ref, packed, *refs, order):
    blocks, out_ref, sems = refs[: len(order)], refs[-2], refs[-1]
    f = f_ref[0]
    copies = [pltpu.make_async_copy(packed.at[f], out_ref.at[f], sems.at[0])]
    for k, r in enumerate(order):
        copies.append(pltpu.make_async_copy(blocks[k], out_ref.at[f ^ r], sems.at[k + 1]))
    for copy in copies:
        copy.start()
    for copy in copies:
        copy.wait()


def assemble(f, packed, blocks, order):
    return pl.pallas_call(
        functools.partial(assemble_kernel, order=order),
        in_specs=[pl.BlockSpec(memory_space=pltpu.SMEM)]
        + [pl.BlockSpec(memory_space=pl.ANY)] * (1 + len(blocks)),
        out_specs=pl.BlockSpec(memory_space=pltpu.VMEM),
        out_shape=jax.ShapeDtypeStruct(packed.shape, packed.dtype),
        scratch_shapes=[pltpu.SemaphoreType.DMA((1 + len(blocks),))],
        name="assemble_rows",
    )(f, packed, *blocks)


def together(*values):
    return lax.optimization_barrier(values)


def scale_of(u):
    return lax.rsqrt(jnp.mean(u * u, axis=-1, keepdims=True) + EPSILON)


def split_two(v):
    high = lax.reduce_precision(v, 8, 7)
    return high.astype(BF16), (v - high).astype(BF16)


def steps(
    hidden, d_out, seg_ids, w_in, w_out, norm_in, norm_gate, conv_w, conv_b, dt_bias, a_log, d_skip
):
    fs, cp = lax.axis_size("fsdp"), lax.axis_size("cp")
    f = lax.axis_index("fsdp")
    width = hidden.shape[-1]
    heads = HEADS // fs
    nh = heads + heads % 2
    hc, hp = heads * HEADDIM, nh * HEADDIM
    wid = 2 * hp + 2 * STATE + LANES
    rows_in = width // fs
    cps = cp
    per = fs // cp
    planes = [k // 2 if k % 2 == 0 else cp - 1 - k // 2 for k in range(cp)]
    there = [
        (a * cp + b, ((a // cp) * cp + b) * cp + planes[a % cp])
        for a in range(fs)
        for b in range(cp)
    ]
    back = [(b, a) for a, b in there]
    base = f.astype(jnp.int32).reshape(1)

    def move(a, route):
        return lax.ppermute(a, ("fsdp", "cp"), route)

    first = hidden.reshape(GROUP, width)
    scale = scale_of(first)
    normed = lax.reduce_precision(first * scale * norm_in[0], 8, 7)
    high, low = split_two(1.0 / scale)

    def rebuilt(normed, high, low):
        return normed.astype(F32) * (high.astype(F32) + low.astype(F32)) / norm_in[0]

    left_over = (first - rebuilt(normed, high, low)).astype(BF16)
    normed = normed.astype(BF16)
    marks = pad_to(
        jnp.concatenate([seg_ids.reshape(GROUP, 1).astype(BF16), high, low], axis=1), 1, LANES
    )
    moved = move(jnp.concatenate([normed, marks], axis=1), there)
    own_scale = moved[:, width + 1 : width + 3]
    own_normed = moved[:, :width]
    marked, _ = gather_plane(moved)
    normed_all = marked[:, :width]
    marks = marked[:, width].astype(F32).reshape(fs, GROUP)
    natural = [place_of(jnp.asarray(k) ^ f, fs) for k in range(fs)]
    segs = jnp.stack(
        [lax.dynamic_index_in_dim(marks, n, 0, False) for n in natural]
    ).reshape(per, cps * GROUP)
    total = per * cps * GROUP
    place = jnp.arange(cps * GROUP)
    cols = []
    for k in (1, 2, 3):
        before = jnp.roll(segs, k, axis=1)
        cols.append(jnp.logical_and(before == segs, place[None, :] >= k).astype(F32))
    grouped = segs.reshape(per, cps, GROUP)
    before = jnp.concatenate([segs[:, :1], grouped[:, :-1, -1]], axis=1)
    keep = (grouped == before[:, :, None]).astype(F32)
    tail = (grouped == grouped[:, :, -1:]).astype(F32)
    cols += [keep, tail, grouped, jnp.broadcast_to(keep[:, :, -1:], keep.shape)]
    meta = pad_to(jnp.stack([c.reshape(total) for c in cols], axis=1), 1, LANES)
    seg_rows = jnp.broadcast_to(segs.reshape(1, total), (8, total))
    ex = (jnp.arange(hp)[None, :] // HEADDIM == jnp.arange(LANES)[:, None]).astype(BF16)

    eye = jnp.eye(LANES, dtype=BF16)

    def send_in(packed):
        return [
            swap(lax.dynamic_index_in_dim(packed, f ^ r, 0, False), "fsdp", r)
            for r in far_first(fs)
        ]

    def place_in(packed, blocks):
        return assemble(base, packed, blocks, far_first(fs)).reshape(width, wid)

    def finish_out(got):
        out_w = pad_to(got.transpose(1, 0, 2).reshape(hc, width), 0, hp)
        return jnp.concatenate(
            [
                pad_to(out_w, 1, width + LANES),
                jnp.concatenate([jnp.zeros((LANES, width), BF16), eye], axis=1),
            ],
            axis=0,
        )

    def gather_cp(a):
        return lax.all_gather(a, "cp", axis=0)

    got_in, got_out = [None] * LAYERS, [None] * LAYERS
    got_in[0] = gather_cp(w_in[0])
    last_grad = d_out.reshape(GROUP, width)
    got_in[0], left_over = together(got_in[0], left_over)
    packed = pack(jnp.zeros((1,), F32), got_in[0], wid, fs, cp)
    left_over = move(left_over, there)
    full_in, full_out = [place_in(packed, send_in(packed))], []
    for i in range(LAYERS):
        if i:
            got_in[i] = gather_cp(w_in[i])
        got_out[i] = gather_cp(w_out[i])

    def own(v, size, padded):
        return pad_to(lax.dynamic_slice_in_dim(v, f * size, size, v.ndim - 1), v.ndim - 1, padded)

    params = []
    for i in range(LAYERS):
        taps = jnp.concatenate([conv_w[i], conv_b[i][None]], axis=0)
        cw = jnp.concatenate([own(taps[:, :INNER], hc, hp), taps[:, INNER:]], axis=1)
        rate = -jnp.exp(own(a_log[i], heads, heads))
        dtp = jnp.stack([own(dt_bias[i], heads, LANES), pad_to(rate, 0, LANES)])
        skip = own(jnp.repeat(d_skip[i], HEADDIM), hc, hp)
        chp = jnp.stack([skip, own(norm_gate[i], hc, hp)])
        params.append((pad_to(cw, 0, 8), pad_to(dtp, 0, 8), pad_to(chp, 0, 8), ex))

    saved = []
    sizes = dict(hp=hp, nh=nh, cps=cps)
    added = 0.0
    for i in range(LAYERS):
        if i:
            normed = (current * scale_of(current) * norm_in[i]).astype(BF16)
            normed_all, blocks = gather_plane(normed, blocks)
            full_in.append(place_in(packed, blocks))
        project = mm(normed_all, full_in[i], 1, 0)
        if i + 1 < LAYERS:
            packed = pack(project[0, :1], got_in[i + 1], wid, fs, cp)
            project, packed = together(project, packed)
            blocks = send_in(packed)
        if i + 1 == LAYERS:
            project, last_grad = together(project, last_grad)
            moved_grad = move(last_grad.astype(BF16), there)
        rg, y, states = ssd_forward(base, project, meta, seg_rows, *params[i], **sizes)
        rg, got_out[i] = together(rg, got_out[i])
        full_out.append(finish_out(got_out[i]))
        summed, *_ = scatter_plane(rg, full_out[i], 0, width // 2)
        inv = lax.rsqrt(
            jnp.sum(summed[:, width:], axis=1, keepdims=True) * (1.0 / INNER) + EPSILON
        )
        branch = summed[:, :width] * inv
        if i == 0:
            current = rebuilt(own_normed, own_scale[:, :1], own_scale[:, 1:]) + left_over
        saved.append((current, normed_all, project, y, states, branch, inv))
        current = current + branch
        added = added + branch
    activations = first + move(added.astype(BF16), back).astype(F32)

    grads_in, grads_out, small = [None] * LAYERS, [None] * LAYERS, [None] * LAYERS
    norm_sums = {}
    change = 0.0
    waiting = None

    def send_out(d_wi):
        blocks = {0: lax.dynamic_index_in_dim(d_wi, f, 0, False)}
        for r in far_first(fs):
            blocks[r] = swap(lax.dynamic_index_in_dim(d_wi, f ^ r, 0, False), "fsdp", r)
        return [blocks[r] for r in range(fs)]

    def sum_in(wide):
        wide = lax.psum_scatter(wide, "cp", scatter_dimension=0, tiled=True)
        return wide[0].astype(F32)

    for i in reversed(range(LAYERS)):
        before, normed_all, project, y, states, branch, inv = saved[i]
        grad_b = (moved_grad.astype(F32) + change).astype(BF16)
        dots = jnp.sum(branch * grad_b.astype(F32), axis=1, keepdims=True)
        scal = jnp.concatenate([*split_two(inv), *split_two(dots)], axis=1)
        payload = jnp.concatenate([grad_b, pad_to(scal, 1, LANES)], axis=1)
        if waiting is not None:
            payload, waiting = gather_plane(payload, waiting)
            wide = unpack(base, send_out(waiting[0]), hp, fs, cp)
        else:
            payload, _ = gather_plane(payload)
        gx = mm(payload, full_out[i], 1, 1)
        gp, gated, gcw, gch, gdt = ssd_backward(
            base, project, meta, seg_rows, *params[i], y, states, gx, **sizes
        )
        rate = -jnp.exp(own(a_log[i], heads, heads))
        by_head = jnp.sum(gch[0, :hc].reshape(heads, HEADDIM), axis=1)
        thin = jnp.concatenate([gdt[0, :heads], gdt[1, :heads] * rate, by_head])
        rows = [gcw[:5], gch[1:2], thin[None]]
        rows += [norm_sums[i + 1][None]] if i + 1 < LAYERS else [thin[None]]
        small[i] = jnp.concatenate([pad_to(row, 1, width) for row in rows], axis=0)
        if waiting is not None:
            tables = sum_over("cp", jnp.stack(small))
            gp, wide, grads_out[i + 1], tables = together(gp, wide, grads_out[i + 1], tables)
            grads_in[i + 1] = sum_in(wide)
        d_wi = mm(normed_all, gp, 0, 0).astype(BF16).reshape(fs, rows_in, wid)
        d_wo = mm(gated[:, :hc], payload[:, :width], 0, 0).astype(BF16)
        if i:
            g_normed, d_wo, waiting, _ = scatter_plane(
                gp, full_in[i], 1, width // 2, (d_wo, [d_wi])
            )
        else:
            gp, d_wi, d_wo = together(gp, d_wi, d_wo)
            blocks = send_out(d_wi)
            g_normed, tables, blocks, _ = scatter_plane(
                gp, full_in[i], 1, width // 2, (tables, blocks)
            )
        d_wo = d_wo.reshape(hc, cp, width // cp).transpose(1, 0, 2)
        d_wo = lax.psum_scatter(d_wo, "cp", scatter_dimension=0, tiled=True)
        grads_out[i] = d_wo[0].astype(F32)
        if i == 0:
            wide = unpack(base, blocks, hp, fs, cp)
            wide, grads_in[i + 1] = together(wide, grads_in[i + 1])
            grads_in[i] = sum_in(wide)

        scale = scale_of(before)
        hat = before * scale
        pulled = g_normed * norm_in[i]
        change = change + scale * (pulled - hat * jnp.mean(pulled * hat, axis=-1, keepdims=True))
        norm_sums[i] = jnp.sum(g_normed * hat, axis=0)

    d_hidden = last_grad + move(change.astype(BF16), back).astype(F32)
    shape = hidden.shape
    first_norm = jnp.broadcast_to(norm_sums[0].reshape(1, -1, LANES), (1, width // LANES, LANES))
    first_norm = sum_over("cp", sum_over("fsdp", first_norm)).reshape(1, width)
    full = jnp.zeros((LAYERS, 8, CHANNELS), F32)
    full = lax.dynamic_update_slice(full, tables[:, :6, :hc], (0, 0, f * hc))
    full = full.at[:, :5, INNER:].set(tables[:, :5, hp : hp + 2 * STATE])
    thin = tables[:, 6, : 3 * heads].reshape(LAYERS, 3, heads)
    thin = lax.dynamic_update_slice(jnp.zeros((LAYERS, 3, HEADS), F32), thin, (0, 0, f * heads))
    full = full.at[:, 6, : 3 * HEADS].set(thin.reshape(LAYERS, 3 * HEADS))
    full = full.at[:-1, 7, :width].set(tables[:-1, 7])
    tables = sum_over("fsdp", full)
    thin = tables[:, 6, : 3 * HEADS].reshape(LAYERS, 3, HEADS)
    return (
        activations.reshape(shape),
        d_hidden.reshape(shape),
        jnp.stack(grads_in),
        jnp.stack(grads_out),
        jnp.concatenate([first_norm, tables[:-1, 7, :width]], axis=0),
        tables[:, 5, :INNER],
        tables[:, :4],
        tables[:, 4],
        thin[:, 0],
        thin[:, 1],
        thin[:, 2],
    )


def solution(mesh):
    in_specs = (
        P("fsdp", "cp", None),
        P("fsdp", "cp", None),
        P("fsdp", "cp"),
        P(None, "fsdp", "cp"),
        P(None, "fsdp", "cp"),
    ) + (P(),) * 7
    out_specs = (
        P("fsdp", "cp", None),
        P("fsdp", "cp", None),
        P(None, "fsdp", "cp"),
        P(None, "fsdp", "cp"),
    ) + (P(),) * 7
    return jax.shard_map(steps, mesh=mesh, in_specs=in_specs, out_specs=out_specs, check_vma=False)
```
